128 devices in a mesh: modes: 4 (over z_lo, core), rows: 32 (over x, z_hi, y).
Axes of the slice: x: 4, y: 4, z: 4 (z_hi: 2, z_lo: 2; z = z_hi * 2 + z_lo), core: 2. Of those that a mesh axis runs over, the one named last changes fastest.
Arguments:
- screens: float32 [2, 2048, 2048], P(None, 'rows'), may hold values from -6 to 6
- weights: float32 [8], P('modes'), may hold values from 0.05 to 0.5
Outputs:
- irradiance: float32 [2048, 2048], P('rows', 'modes')
The draws below stay inside these ranges and needn't reach their ends.
All inputs are finite; a program needn't handle non-finite values.
Results may differ from the reference program's by a relative error of at most 0.0001.
Values sent between devices are 32-bit elements; how exact they have to be, the bound alone decides.
No kernel may reach another device: no remote copies, remote signals or barrier semaphores. Data moves between devices by JAX's collectives and lax.ppermute only.
A program may use at most 128 MiB of HBM per device.

```python
import math
import jax
import jax.numpy as jnp

N = 2048
MODES = 8
STEPS = 2


def steps_of(key, shape, split, least, largest):
    def one(dim, blocks):
        heights = jax.random.uniform(jax.random.fold_in(jax.random.fold_in(key, 6), dim), (blocks,), jnp.float32, least / len(split), largest / len(split))
        return jnp.repeat(jnp.exp(heights), shape[dim] // blocks).reshape((-1,) + (1,) * (len(shape) - dim - 1))

    level = one(*split[0])
    for cut in split[1:]:
        level = level * one(*cut)
    return level


def noise(key, extent, width, most, split=(), kind=jnp.bfloat16):
    loudness = steps_of(key, extent, split, -0.22, 0.18) if split else 1.0
    values = jax.random.normal(key, extent, jnp.float32) * width * loudness
    return jnp.minimum(jnp.maximum(values, -most), most).astype(kind)


def setup_inputs(seed: int = 0) -> dict:
    splits = jax.random.split(jax.random.key(seed), 3)
    screens = noise(splits[0], (STEPS, N, N), 1.0, 6.0, ((1, 32),), jnp.float32)
    weights = jnp.clip(jnp.exp(math.log(0.5) - 2.3025851 * jax.random.uniform(splits[1], (MODES,), jnp.float32) ** steps_of(splits[1], (MODES,), ((0, 4),), -0.2, 0.2)), 0.05, 0.5)
    return {"screens": screens, "weights": weights}


beam_amplitude = math.sqrt(8.0 / math.sqrt(math.pi / 2.0))

def hermite_rows(coord, count):
    scaled = coord * math.sqrt(2.0)
    polys = [jnp.ones_like(coord), 2.0 * scaled]
    for level in range(1, count - 1):
        polys.append(2.0 * scaled * polys[level] - 2.0 * level * polys[level - 1])
    envelope = jnp.exp(-coord * coord) * beam_amplitude
    result = []
    for level in range(count):
        norm_value = math.sqrt(2.0 ** level * math.factorial(level))
        result.append(polys[level] * envelope / norm_value)
    return result

def reference(screens, weights):
    cells = jnp.arange(N, dtype=jnp.int32)
    coord = (cells.astype(jnp.float32) - (N / 2 - 0.5)) / (N / 8)
    count = max(4, (MODES - 1) // 4 + 1)
    table = hermite_rows(coord, count)
    signed = jnp.where(cells >= N // 2, cells - N, cells)
    square = signed * signed
    residue = (square[:, None] + square[None, :]) % (8 * N)
    angle = residue.astype(jnp.float32) * (-2.0 * math.pi / (8 * N))
    kernel = jnp.cos(angle) + 1j * jnp.sin(angle)
    total = jnp.zeros((N, N), jnp.float32)
    for mode in range(MODES):
        field = table[mode // 4][:, None] * table[mode % 4][None, :]
        for step in range(STEPS):
            field = field * jnp.exp(1j * screens[step])
            field = jnp.fft.ifft2(jnp.fft.fft2(field) * kernel)
        real_part = jnp.real(field)
        imag_part = jnp.imag(field)
        total = total + weights[mode] * (real_part * real_part + imag_part * imag_part)
    return total
```

```python
import math

import jax
import jax.numpy as jnp
import numpy as np
from jax import lax
from jax.experimental import pallas as pl
from jax.experimental.pallas import tpu as pltpu
from jax.sharding import PartitionSpec as P

N = 2048
RADIX = 8
BLOCK = N // RADIX
LANES = 128
GROUP = 16
MSG = 20
BOTH = ("rows", "modes")
AMPLITUDE = math.sqrt(8.0 / math.sqrt(math.pi / 2.0))
HALF = math.sqrt(0.5)


def block_tables():
    freq = np.arange(N)
    signed = np.where(freq >= N // 2, freq - N, freq)
    transfer = np.exp(-2j * np.pi * ((signed * signed) % (8 * N)) / (8 * N))
    offset = np.arange(384)[:, None] - 128 - np.arange(LANES)[None, :]
    bands = np.zeros((RADIX, 2, 384, LANES), np.float64)
    for j in range(RADIX):
        shifted = np.zeros(N, np.complex128)
        shifted[j::RADIX] = transfer[j::RADIX]
        impulse = np.fft.ifft(shifted)
        band = impulse[offset % N]
        bands[j, 0] = band.real
        bands[j, 1] = band.imag
    high = bands.astype(np.float32).astype(jnp.bfloat16)
    low = (bands - high.astype(np.float64)).astype(np.float32).astype(jnp.bfloat16)
    return high, low


def profile_table():
    coord = (np.arange(N) - (N / 2 - 0.5)) / (N / 8)
    scaled = coord * math.sqrt(2.0)
    polys = [np.ones_like(coord), 2.0 * scaled]
    for level in range(1, 3):
        polys.append(2.0 * scaled * polys[level] - 2.0 * level * polys[level - 1])
    rows = []
    for level in range(4):
        norm = math.sqrt(2.0**level * math.factorial(level))
        rows.append(polys[level] * np.exp(-coord * coord) * AMPLITUDE / norm)
    return np.stack(rows).astype(np.float32).reshape(4, 1, N)


def butterfly(x):
    def add(u, v):
        return (u[0] + v[0], u[1] + v[1])

    def sub(u, v):
        return (u[0] - v[0], u[1] - v[1])

    def down(u):
        return (u[1], -u[0])

    a = [add(x[q], x[q + 4]) for q in range(4)]
    b = [sub(x[q], x[q + 4]) for q in range(4)]
    c0, c1 = add(a[0], a[2]), sub(a[0], a[2])
    d0, d1 = add(a[1], a[3]), down(sub(a[1], a[3]))
    e1 = ((b[1][0] + b[1][1]) * HALF, (b[1][1] - b[1][0]) * HALF)
    e3 = ((b[3][1] - b[3][0]) * HALF, (b[3][0] + b[3][1]) * -HALF)
    e2 = down(b[2])
    f0, f1 = add(b[0], e2), sub(b[0], e2)
    g0, g1 = add(e1, e3), down(sub(e1, e3))
    return [
        add(c0, d0),
        add(f0, g0),
        add(c1, d1),
        add(f1, g1),
        sub(c0, d0),
        sub(f0, g0),
        sub(c1, d1),
        sub(f1, g1),
    ]


def unbutterfly(y):
    return [(z[1], z[0]) for z in butterfly([(v[1], v[0]) for v in y])]


def sincos(x):
    turns = jnp.floor(x * (2.0 / math.pi) + 0.5)
    r = x - turns * 1.5703125
    r = r - turns * 4.837512969970703125e-4
    r = r - turns * 7.54978995489188216e-8
    quadrant = turns.astype(jnp.int32)
    z = r * r
    s = ((-1.9515295891e-4 * z + 8.3321608736e-3) * z - 1.6666654611e-1) * z * r + r
    c = ((2.443315711809948e-5 * z - 1.388731625493765e-3) * z + 4.166664568298827e-2) * z * z
    c = c - 0.5 * z + 1.0
    odd = (quadrant & 1) == 1
    sine = jnp.where(odd, c, s)
    cosine = jnp.where(odd, s, c)
    sine = jnp.where((quadrant & 2) == 2, -sine, sine)
    cosine = jnp.where(((quadrant + 1) & 2) == 2, -cosine, cosine)
    return sine, cosine


def split(value):
    high = value.astype(jnp.bfloat16)
    low = (value - high.astype(jnp.float32)).astype(jnp.bfloat16)
    return high, low


def lane_groups(shape):
    return lax.broadcasted_iota(jnp.int32, shape, 1) // GROUP


def swap_groups(rows):
    rows = list(rows)
    groups = lane_groups(rows[0].shape)
    for step in (1, 2, 4):
        keep = (groups & step) == 0
        for k in range(8):
            if k & step == 0:
                low, high = rows[k], rows[k + step]
                rows[k] = jnp.where(keep, low, pltpu.roll(high, step * GROUP, 1))
                rows[k + step] = jnp.where(
                    keep, pltpu.roll(low, LANES - step * GROUP, 1), high
                )
    return rows


def matrix(table_ref, j, part):
    return jnp.concatenate(
        [table_ref[j, part, 128:384, :], table_ref[j, part, 0:256, :]], axis=1
    )


def dot(left, right):
    return jnp.dot(left, right, preferred_element_type=jnp.float32)


def blocks_on_lanes(half, zh_ref, zl_ref, hi_ref, lo_ref, y_ref):
    def body(j, carry):
        t = lax.rem(RADIX - j, RADIX)
        zh, zl = zh_ref[j], zl_ref[j]
        wrh, wih = matrix(hi_ref, t, 0), matrix(hi_ref, t, 1)
        wrl, wil = matrix(lo_ref, t, 0), matrix(lo_ref, t, 1)
        pr = dot(zh, wrh) + dot(zl, wrh) + dot(zh, wrl)
        pi = dot(zh, wih) + dot(zl, wih) + dot(zh, wil)
        y_ref[j, 0] = pr[:half] - pi[half:]
        y_ref[j, 1] = pi[:half] + pr[half:]
        return carry

    lax.fori_loop(0, RADIX, body, 0)


def blocks_on_sublanes(zh_ref, zl_ref, hi_ref, lo_ref, y_ref):
    def body(j, carry):
        zh, zl = zh_ref[j], zl_ref[j]
        brh, bih = matrix(hi_ref, j, 0), matrix(hi_ref, j, 1)
        brl, bil = matrix(lo_ref, j, 0), matrix(lo_ref, j, 1)
        tr = dot(brh, zh) + dot(brh, zl) + dot(brl, zh)
        ti = dot(bih, zh) + dot(bih, zl) + dot(bil, zh)
        y_ref[j, 0] = tr[:, :LANES] - ti[:, LANES:]
        y_ref[j, 1] = tr[:, LANES:] + ti[:, :LANES]
        return carry

    lax.fori_loop(0, RADIX, body, 0)


def first_kernel(
    screens_ref, prof_ref, hi_ref, lo_ref, out_ref, cs_ref, e_ref, zh_ref, zl_ref, y_ref, t_ref
):
    m = lax.axis_index("modes")
    r = lax.axis_index("rows")
    rows = pl.ds(pl.multiple_of(m * 16, 16), 16)
    cell = lax.broadcasted_iota(jnp.int32, (16, LANES), 0) + (r * 64 + m * 16)
    coord = (cell.astype(jnp.float32) - (N / 2 - 0.5)) / (N / 8)
    envelope = jnp.exp(-coord * coord) * AMPLITUDE

    def screens(t, carry):
        lanes = pl.ds(pl.multiple_of(t * LANES, LANES), LANES)
        sine, cosine = sincos(screens_ref[0, rows, lanes])
        cs_ref[0, t] = cosine * envelope
        cs_ref[1, t] = sine * envelope
        sine, cosine = sincos(screens_ref[1, rows, lanes])
        e_ref[t, 0] = cosine
        e_ref[t, 1] = sine
        return carry

    lax.fori_loop(0, 16, screens, 0)

    def forward(i, carry):
        b, h = i // 2, i % 2
        lanes = pl.ds(pl.multiple_of(h * LANES, LANES), LANES)
        xs = []
        for q in range(RADIX):
            at = pl.ds(pl.multiple_of(q * BLOCK + h * LANES, LANES), LANES)
            weight = prof_ref[b, :, at]
            xs.append((cs_ref[0, q * 2 + h] * weight, cs_ref[1, q * 2 + h] * weight))
        for j, pair in enumerate(butterfly(xs)):
            for c in range(2):
                at = pl.ds(pl.multiple_of(c * 64 + b * 16, 16), 16)
                high, low = split(pair[c])
                zh_ref[j, at, lanes] = high
                zl_ref[j, at, lanes] = low
        return carry

    lax.fori_loop(0, 8, forward, 0)
    blocks_on_lanes(64, zh_ref, zl_ref, hi_ref, lo_ref, y_ref)

    def backward(i, carry):
        b, h = i // 2, i % 2
        lanes = pl.ds(pl.multiple_of(h * LANES, LANES), LANES)
        at = pl.ds(pl.multiple_of(b * 16, 16), 16)
        ys = [(y_ref[j, 0, at, lanes], y_ref[j, 1, at, lanes]) for j in range(RADIX)]
        for q, pair in enumerate(unbutterfly(ys)):
            t_ref[q * 2 + h, b] = pair[0]
            t_ref[q * 2 + h, 4 + b] = pair[1]
        return carry

    lax.fori_loop(0, 8, backward, 0)
    parity = m % 2

    def pack(t, carry):
        base = t * (8 * MSG)
        fields = swap_groups([t_ref[t, k] for k in range(8)])
        phases = swap_groups(
            [e_ref[t, k % 2, pl.ds(k // 2, 4, stride=4), :] for k in range(8)]
        )
        for k in range(8):
            out_ref[pl.ds(base + k * MSG + parity * 4, 16), :] = fields[k]
            out_ref[pl.ds(base + k * MSG + (1 - parity) * 16, 4), :] = phases[k]
        return carry

    lax.fori_loop(0, 16, pack, 0)


def second_kernel(in_ref, hi_ref, lo_ref, out_ref, e_ref, zh_ref, zl_ref, y_ref):
    groups = lane_groups((8, LANES))

    def phases(p, carry):
        packed = in_ref[pl.ds(pl.multiple_of(p * 40 + 16, 8), 8), :]
        level = [packed]
        for step in (4, 2, 1):
            keep = (groups & step) == 0
            following = []
            for value in level:
                moved = pltpu.roll(value, step * GROUP, 1)
                following.append(jnp.where(keep, value, moved))
                following.append(jnp.where(keep, moved, value))
            level = following
        for k in range(8):
            e_ref[k % 2, pl.ds(p * 32 + k // 2, 8, stride=4), :] = level[k]
        return carry

    lax.fori_loop(0, 64, phases, 0)
    left = lax.broadcasted_iota(jnp.int32, (16, LANES), 1) < 64
    line = lax.broadcasted_iota(jnp.int32, (16, LANES), 0)

    def store(at, pairs):
        for j, pair in enumerate(pairs):
            for c in range(2):
                high, low = split(pair[c])
                zh_ref[j, at, c * LANES : (c + 1) * LANES] = high
                zl_ref[j, at, c * LANES : (c + 1) * LANES] = low

    def load(at):
        return unbutterfly([(y_ref[j, 0, at, :], y_ref[j, 1, at, :]) for j in range(RADIX)])

    def forward(p, carry):
        for u in range(2):
            xs = []
            for q in range(RADIX):
                row = pl.multiple_of(p * 40 + (q * 320 + u * 24), 8)
                value = in_ref[pl.ds(row, 16), :]
                moved = pltpu.roll(value, 64, 1)
                cell = (line + (q * BLOCK + u * 16 + p * 32)).astype(jnp.float32)
                factor = jnp.where(left, 1.0, (cell - (N / 2 - 0.5)) * (2.0 / (N / 8)))
                xs.append((jnp.where(left, value, moved) * factor, jnp.where(left, moved, value) * factor))
            store(pl.ds(pl.multiple_of(p * 32 + u * 16, 16), 16), butterfly(xs))
        return carry

    lax.fori_loop(0, 8, forward, 0)
    blocks_on_sublanes(zh_ref, zl_ref, hi_ref, lo_ref, y_ref)

    def middle(s, carry):
        at = pl.ds(pl.multiple_of(s * 16, 16), 16)
        xs = []
        for q, (re, im) in enumerate(load(at)):
            here = pl.ds(pl.multiple_of(s * 16 + q * BLOCK, 16), 16)
            cosine, sine = e_ref[0, here, :], e_ref[1, here, :]
            xs.append((re * cosine - im * sine, re * sine + im * cosine))
        store(at, butterfly(xs))
        return carry

    lax.fori_loop(0, 16, middle, 0)
    blocks_on_sublanes(zh_ref, zl_ref, hi_ref, lo_ref, y_ref)

    def backward(s, carry):
        at = pl.ds(pl.multiple_of(s * 16, 16), 16)
        for q, (re, im) in enumerate(load(at)):
            row = pl.multiple_of(s * 32 + q * 512, 32)
            out_ref[pl.ds(row, 16), :] = re
            out_ref[pl.ds(row + 16, 16), :] = im
        return carry

    lax.fori_loop(0, 16, backward, 0)


def third_kernel(
    in_ref, weight_ref, hi_ref, lo_ref, out0, out1, out2, out3, t_ref, zh_ref, zl_ref, y_ref, i_ref
):
    m = lax.axis_index("modes")

    def unpack(t, carry):
        for c in range(2):
            values = [
                in_ref[pl.ds(pl.multiple_of(t * 256 + (s * 32 + c * 16), 16), 16), :]
                for s in range(8)
            ]
            for k, value in enumerate(swap_groups(values)):
                t_ref[t, c, k] = value
        return carry

    lax.fori_loop(0, 16, unpack, 0)

    def forward(i, carry):
        mode, h = i // 2, i % 2
        lanes = pl.ds(pl.multiple_of(h * LANES, LANES), LANES)
        xs = [(t_ref[q * 2 + h, 0, mode], t_ref[q * 2 + h, 1, mode]) for q in range(RADIX)]
        for j, pair in enumerate(butterfly(xs)):
            for c in range(2):
                at = pl.ds(pl.multiple_of(c * 128 + mode * 16, 16), 16)
                high, low = split(pair[c])
                zh_ref[j, at, lanes] = high
                zl_ref[j, at, lanes] = low
        return carry

    lax.fori_loop(0, 16, forward, 0)
    blocks_on_lanes(128, zh_ref, zl_ref, hi_ref, lo_ref, y_ref)
    for t in range(16):
        i_ref[t] = jnp.zeros((16, LANES), jnp.float32)

    def backward(i, carry):
        mode, h = i // 2, i % 2
        lanes = pl.ds(pl.multiple_of(h * LANES, LANES), LANES)
        at = pl.ds(pl.multiple_of(mode * 16, 16), 16)
        weight = weight_ref[jnp.bitwise_xor(m, mode // 2), mode % 2]
        ys = [(y_ref[j, 0, at, lanes], y_ref[j, 1, at, lanes]) for j in range(RADIX)]
        for q, (re, im) in enumerate(unbutterfly(ys)):
            i_ref[q * 2 + h] += weight * (re * re + im * im)
        return carry

    lax.fori_loop(0, 16, backward, 0)
    for k, out_ref in enumerate((out0, out1, out2, out3)):
        owner = jnp.bitwise_xor(m, k)
        for t in range(4):
            out_ref[:, t * LANES : (t + 1) * LANES] = i_ref[owner * 4 + t]


def last_kernel(in0, in1, in2, in3, out_ref):
    m = lax.axis_index("modes")
    for k, in_ref in enumerate((in0, in1, in2, in3)):
        row = pl.multiple_of(jnp.bitwise_xor(m, k) * 16, 16)
        out_ref[pl.ds(row, 16), :] = in_ref[...]


def f32(*shape):
    return jax.ShapeDtypeStruct(shape, jnp.float32)


def exchange(value):
    return lax.all_to_all(value, BOTH, split_axis=0, concat_axis=0, tiled=True)


def partner(value, k):
    return lax.ppermute(value, "modes", [(i, i ^ k) for i in range(4)])


def shards(screens, weights):
    high, low = (jnp.asarray(table) for table in block_tables())
    profiles = jnp.asarray(profile_table())
    vmem = pl.BlockSpec(memory_space=pltpu.VMEM)
    smem = pl.BlockSpec(memory_space=pltpu.SMEM)
    z_scratch = [pltpu.VMEM((RADIX, 256, 256), jnp.bfloat16)] * 2

    mine = weights.reshape(1, 2)
    everyone = jnp.concatenate([mine] + [partner(mine, k) for k in (1, 2, 3)])

    sent = pl.pallas_call(
        first_kernel,
        out_shape=f32(128 * MSG, LANES),
        in_specs=[vmem] * 4,
        out_specs=vmem,
        scratch_shapes=[
            pltpu.VMEM((2, 16, 16, LANES), jnp.float32),
            pltpu.VMEM((16, 2, 16, LANES), jnp.float32),
            pltpu.VMEM((RADIX, 128, 256), jnp.bfloat16),
            pltpu.VMEM((RADIX, 128, 256), jnp.bfloat16),
            pltpu.VMEM((RADIX, 2, 64, 256), jnp.float32),
            pltpu.VMEM((16, 8, 16, LANES), jnp.float32),
        ],
        name="first",
    )(screens, profiles, high, low)
    got = exchange(sent.reshape(128 * MSG, 1, LANES)).reshape(128 * MSG, LANES)

    sent = pl.pallas_call(
        second_kernel,
        out_shape=f32(128 * 32, LANES),
        in_specs=[vmem] * 3,
        out_specs=vmem,
        scratch_shapes=[pltpu.VMEM((2, N, LANES), jnp.float32)]
        + z_scratch
        + [pltpu.VMEM((RADIX, 2, 256, LANES), jnp.float32)],
        name="second",
    )(got, high, low)
    got = exchange(sent.reshape(128, 32, LANES)).reshape(128 * 32, LANES)

    pieces = pl.pallas_call(
        third_kernel,
        out_shape=[f32(16, 512)] * 4,
        in_specs=[vmem, smem, vmem, vmem],
        out_specs=[vmem] * 4,
        scratch_shapes=[pltpu.VMEM((16, 2, 8, 16, LANES), jnp.float32)]
        + z_scratch
        + [
            pltpu.VMEM((RADIX, 2, 128, 256), jnp.float32),
            pltpu.VMEM((16, 16, LANES), jnp.float32),
        ],
        name="third",
    )(got, everyone, high, low)
    pieces = [pieces[0]] + [partner(pieces[k], k) for k in (1, 2, 3)]

    return pl.pallas_call(
        last_kernel,
        out_shape=f32(64, 512),
        in_specs=[vmem] * 4,
        out_specs=vmem,
        name="last",
    )(*pieces)


def solution(mesh):
    return jax.shard_map(
        shards,
        mesh=mesh,
        in_specs=(P(None, "rows", None), P("modes")),
        out_specs=P("rows", "modes"),
        check_vma=False,
    )
```

```python
import math

import jax
import jax.numpy as jnp
import numpy as np
from jax import lax
from jax.experimental import pallas as pl
from jax.experimental.pallas import tpu as pltpu
from jax.sharding import PartitionSpec as P

N = 2048
RADIX = 8
BLOCK = N // RADIX
LANES = 128
GROUP = 16
MSG = 18
BOTH = ("rows", "modes")
AMPLITUDE = math.sqrt(8.0 / math.sqrt(math.pi / 2.0))
HALF = math.sqrt(0.5)


def params(mib):
    return pltpu.CompilerParams(vmem_limit_bytes=mib * 2**20)


def block_tables():
    freq = np.arange(N)
    signed = np.where(freq >= N // 2, freq - N, freq)
    transfer = np.exp(-2j * np.pi * ((signed * signed) % (8 * N)) / (8 * N))
    offset = np.arange(384)[:, None] - 128 - np.arange(LANES)[None, :]
    bands = np.zeros((RADIX, 2, 384, LANES), np.float64)
    for j in range(RADIX):
        shifted = np.zeros(N, np.complex128)
        shifted[j::RADIX] = transfer[j::RADIX]
        impulse = np.fft.ifft(shifted)
        band = impulse[offset % N]
        bands[j, 0] = band.real
        bands[j, 1] = band.imag
    high = bands.astype(np.float32).astype(jnp.bfloat16)
    low = (bands - high.astype(np.float64)).astype(np.float32).astype(jnp.bfloat16)
    return high, low


def profile_table():
    coord = (np.arange(N) - (N / 2 - 0.5)) / (N / 8)
    scaled = coord * math.sqrt(2.0)
    polys = [np.ones_like(coord), 2.0 * scaled]
    for level in range(1, 3):
        polys.append(2.0 * scaled * polys[level] - 2.0 * level * polys[level - 1])
    rows = []
    for level in range(4):
        norm = math.sqrt(2.0**level * math.factorial(level))
        rows.append(polys[level] * np.exp(-coord * coord) * AMPLITUDE / norm)
    return np.stack(rows).astype(np.float32).reshape(4, 1, N)


def butterfly(x):
    def add(u, v):
        return (u[0] + v[0], u[1] + v[1])

    def sub(u, v):
        return (u[0] - v[0], u[1] - v[1])

    def down(u):
        return (u[1], -u[0])

    a = [add(x[q], x[q + 4]) for q in range(4)]
    b = [sub(x[q], x[q + 4]) for q in range(4)]
    c0, c1 = add(a[0], a[2]), sub(a[0], a[2])
    d0, d1 = add(a[1], a[3]), down(sub(a[1], a[3]))
    e1 = ((b[1][0] + b[1][1]) * HALF, (b[1][1] - b[1][0]) * HALF)
    e3 = ((b[3][1] - b[3][0]) * HALF, (b[3][0] + b[3][1]) * -HALF)
    e2 = down(b[2])
    f0, f1 = add(b[0], e2), sub(b[0], e2)
    g0, g1 = add(e1, e3), down(sub(e1, e3))
    return [
        add(c0, d0),
        add(f0, g0),
        add(c1, d1),
        add(f1, g1),
        sub(c0, d0),
        sub(f0, g0),
        sub(c1, d1),
        sub(f1, g1),
    ]


def unbutterfly(y):
    return [(z[1], z[0]) for z in butterfly([(v[1], v[0]) for v in y])]


def sincos(x):
    turns = jnp.floor(x * (2.0 / math.pi) + 0.5)
    r = x - turns * 1.5703125
    r = r - turns * 4.837512969970703125e-4
    r = r - turns * 7.54978995489188216e-8
    quadrant = turns.astype(jnp.int32)
    z = r * r
    s = ((-1.9515295891e-4 * z + 8.3321608736e-3) * z - 1.6666654611e-1) * z * r + r
    c = ((2.443315711809948e-5 * z - 1.388731625493765e-3) * z + 4.166664568298827e-2) * z * z
    c = c - 0.5 * z + 1.0
    odd = (quadrant & 1) == 1
    sine = jnp.where(odd, c, s)
    cosine = jnp.where(odd, s, c)
    sine = jnp.where((quadrant & 2) == 2, -sine, sine)
    cosine = jnp.where(((quadrant + 1) & 2) == 2, -cosine, cosine)
    return sine, cosine


def split(value):
    high = value.astype(jnp.bfloat16)
    low = (value - high.astype(jnp.float32)).astype(jnp.bfloat16)
    return high, low


def lane_groups(shape):
    return lax.broadcasted_iota(jnp.int32, shape, 1) // GROUP


def swap_groups(rows):
    groups = lane_groups(rows[0].shape)
    rows = [rows[0]] + [pltpu.roll(rows[k], k * GROUP, 1) for k in range(1, 8)]
    for step in (1, 2, 4):
        moves = (groups & step) != 0
        rows = [jnp.where(moves, rows[(k + step) % 8], rows[k]) for k in range(8)]
    return [rows[0]] + [pltpu.roll(rows[8 - k], LANES - k * GROUP, 1) for k in range(1, 8)]


def matrix(table_ref, j, part):
    return jnp.concatenate(
        [table_ref[j, part, 128:384, :], table_ref[j, part, 0:256, :]], axis=1
    )


def dot(left, right):
    return jnp.dot(left, right, preferred_element_type=jnp.float32)


def blocks_on_lanes(half, zh_ref, zl_ref, hi_ref, lo_ref, y_ref, wait=None):
    def body(j, carry):
        t = lax.rem(RADIX - j, RADIX)
        if wait is not None:
            wait(t)
        zh = jnp.concatenate([zh_ref[j, 0], zh_ref[j, 1]], axis=1)
        zl = jnp.concatenate([zl_ref[j, 0], zl_ref[j, 1]], axis=1)
        wrh, wih = matrix(hi_ref, t, 0), matrix(hi_ref, t, 1)
        wrl, wil = matrix(lo_ref, t, 0), matrix(lo_ref, t, 1)
        both = jnp.concatenate([zh, zl], axis=0)
        pr, pi = dot(both, wrh), dot(both, wih)
        pr = pr[: 2 * half] + pr[2 * half :] + dot(zh, wrl)
        pi = pi[: 2 * half] + pi[2 * half :] + dot(zh, wil)
        re = pr[:half] - pi[half:]
        im = pi[:half] + pr[half:]
        for h in range(2):
            y_ref[j, 0, h] = re[:, h * LANES : (h + 1) * LANES]
            y_ref[j, 1, h] = im[:, h * LANES : (h + 1) * LANES]
        return carry

    lax.fori_loop(0, RADIX, body, 0)


def blocks_on_sublanes(zh_ref, zl_ref, hi_ref, lo_ref, y_ref):
    def body(j, carry):
        zh = jnp.concatenate([zh_ref[j, 0], zh_ref[j, 1]], axis=1)
        zl = jnp.concatenate([zl_ref[j, 0], zl_ref[j, 1]], axis=1)
        brh, bih = matrix(hi_ref, j, 0), matrix(hi_ref, j, 1)
        brl, bil = matrix(lo_ref, j, 0), matrix(lo_ref, j, 1)
        tr = dot(brh, zh) + dot(brl, zh) + dot(brh, zl)
        ti = dot(bih, zh) + dot(bil, zh) + dot(bih, zl)
        y_ref[j, 0] = tr[:, :LANES] - ti[:, LANES:]
        y_ref[j, 1] = tr[:, LANES:] + ti[:, :LANES]
        return carry

    lax.fori_loop(0, RADIX, body, 0)


def first_kernel(
    screens_ref,
    prof_ref,
    hi_hbm,
    lo_hbm,
    out_hbm,
    out_ref,
    s_ref,
    e_ref,
    hi_ref,
    lo_ref,
    cs_ref,
    zh_ref,
    zl_ref,
    y_ref,
    t_ref,
    screen_sems,
    table_sems,
    out_sems,
):
    m = lax.axis_index("modes")
    r = lax.axis_index("rows")
    rows = pl.ds(pl.multiple_of(m * 16, 16), 16)

    def screen_copy(k):
        return pltpu.make_async_copy(
            screens_ref.at[k, rows, :], s_ref.at[k], screen_sems.at[k]
        )

    def table_copies(t):
        return [
            pltpu.make_async_copy(hi_hbm.at[t], hi_ref.at[t], table_sems.at[0, t]),
            pltpu.make_async_copy(lo_hbm.at[t], lo_ref.at[t], table_sems.at[1, t]),
        ]

    for k in range(2):
        screen_copy(k).start()
    for j in range(RADIX):
        for copy in table_copies((RADIX - j) % RADIX):
            copy.start()

    cell = lax.broadcasted_iota(jnp.int32, (16, LANES), 0) + (r * 64 + m * 16)
    coord = (cell.astype(jnp.float32) - (N / 2 - 0.5)) / (N / 8)
    envelope = jnp.exp(-coord * coord) * AMPLITUDE
    screen_copy(0).wait()

    def screens(t, carry):
        lanes = pl.ds(pl.multiple_of(t * LANES, LANES), LANES)
        sine, cosine = sincos(s_ref[0, :, lanes])
        cs_ref[0, t] = cosine * envelope
        cs_ref[1, t] = sine * envelope
        return carry

    lax.fori_loop(0, 16, screens, 0, unroll=4)

    def forward(i, carry):
        b, h = i // 2, i % 2
        xs = []
        for q in range(RADIX):
            at = pl.ds(pl.multiple_of(q * BLOCK + h * LANES, LANES), LANES)
            weight = prof_ref[b, :, at]
            xs.append((cs_ref[0, q * 2 + h] * weight, cs_ref[1, q * 2 + h] * weight))
        for j, pair in enumerate(butterfly(xs)):
            for c in range(2):
                at = pl.ds(pl.multiple_of(c * 64 + b * 16, 16), 16)
                high, low = split(pair[c])
                zh_ref[j, h, at, :] = high
                zl_ref[j, h, at, :] = low
        return carry

    lax.fori_loop(0, 8, forward, 0, unroll=2)

    def wait(t):
        for copy in table_copies(t):
            copy.wait()

    blocks_on_lanes(64, zh_ref, zl_ref, hi_ref, lo_ref, y_ref, wait)

    def backward(i, carry):
        b, h = i // 2, i % 2
        at = pl.ds(pl.multiple_of(b * 16, 16), 16)
        ys = [(y_ref[j, 0, h, at, :], y_ref[j, 1, h, at, :]) for j in range(RADIX)]
        for q, pair in enumerate(unbutterfly(ys)):
            t_ref[q * 2 + h, b] = pair[0]
            t_ref[q * 2 + h, 4 + b] = pair[1]
        return carry

    lax.fori_loop(0, 8, backward, 0, unroll=2)
    screen_copy(1).wait()

    def lines(t, carry):
        lanes = pl.ds(pl.multiple_of(t * LANES, LANES), LANES)
        e_ref[pl.ds(pl.multiple_of(t * 16, 16), 16), :] = s_ref[1, :, lanes]
        return carry

    lax.fori_loop(0, 16, lines, 0, unroll=4)
    for t in range(0, 16, 4):
        values = [e_ref[pl.ds(t * 16 + g, 8, stride=8), :] for g in range(8)]
        for k, value in enumerate(swap_groups(values)):
            for u in range(4):
                at = ((t + u) * 8 + k) * MSG + 16
                out_ref[at : at + 2, :] = value[2 * u : 2 * u + 2, :]

    def sending(t):
        at = pl.ds(pl.multiple_of(t * (8 * MSG), 8), 8 * MSG)
        return pltpu.make_async_copy(out_ref.at[at, :], out_hbm.at[at, :], out_sems.at[t])

    def pack(t, carry):
        for k, value in enumerate(swap_groups([t_ref[t, k] for k in range(8)])):
            out_ref[pl.ds((t * 8 + k) * MSG, 16), :] = value
        sending(t).start()
        return carry

    lax.fori_loop(0, 16, pack, 0, unroll=4)
    for t in range(16):
        sending(t).wait()


def second_kernel(
    in_ref, hi_ref, lo_ref, out_hbm, p_ref, e_ref, zh_ref, zl_ref, y_ref, out_ref, sems
):
    groups = lane_groups((8, LANES))

    def gather(p, carry):
        for u in range(8):
            p_ref[pl.ds(p * 16 + u * 2, 2), :] = in_ref[pl.ds(p * (8 * MSG) + u * MSG + 16, 2), :]
        return carry

    lax.fori_loop(0, 16, gather, 0, unroll=4)

    def phases(p, carry):
        packed = p_ref[pl.ds(pl.multiple_of(p * 8, 8), 8), :]
        sine, cosine = sincos(packed)
        for c, value in enumerate((cosine, sine)):
            level = [value]
            for step in (4, 2, 1):
                keep = (groups & step) == 0
                following = []
                for value in level:
                    moved = pltpu.roll(value, step * GROUP, 1)
                    following.append(jnp.where(keep, value, moved))
                    following.append(jnp.where(keep, moved, value))
                level = following
            for k in range(8):
                e_ref[c, pl.ds(p * 64 + k, 8, stride=8), :] = level[k]
        return carry

    lax.fori_loop(0, 32, phases, 0, unroll=4)
    left = lax.broadcasted_iota(jnp.int32, (16, LANES), 1) < 64
    line = lax.broadcasted_iota(jnp.int32, (16, LANES), 0).astype(jnp.float32)
    line = (line - (N / 2 - 0.5)) * (2.0 / (N / 8))

    def store(at, pairs):
        for j, pair in enumerate(pairs):
            for c in range(2):
                high, low = split(pair[c])
                zh_ref[j, c, at, :] = high
                zl_ref[j, c, at, :] = low

    def load(at):
        return unbutterfly([(y_ref[j, 0, at, :], y_ref[j, 1, at, :]) for j in range(RADIX)])

    def forward(s, carry):
        start = (s * 16).astype(jnp.float32) * (2.0 / (N / 8))
        xs = []
        for q in range(RADIX):
            value = in_ref[pl.ds((s + q * 16) * MSG, 16), :]
            moved = pltpu.roll(value, 64, 1)
            factor = jnp.where(left, 1.0, line + (start + q * BLOCK * (2.0 / (N / 8))))
            xs.append((jnp.where(left, value, moved) * factor, jnp.where(left, moved, value) * factor))
        store(pl.ds(pl.multiple_of(s * 16, 16), 16), butterfly(xs))
        return carry

    lax.fori_loop(0, 16, forward, 0, unroll=2)
    blocks_on_sublanes(zh_ref, zl_ref, hi_ref, lo_ref, y_ref)

    def middle(s, carry):
        at = pl.ds(pl.multiple_of(s * 16, 16), 16)
        xs = []
        for q, (re, im) in enumerate(load(at)):
            here = pl.ds(pl.multiple_of(s * 16 + q * BLOCK, 16), 16)
            cosine, sine = e_ref[0, here, :], e_ref[1, here, :]
            xs.append((re * cosine - im * sine, re * sine + im * cosine))
        store(at, butterfly(xs))
        return carry

    lax.fori_loop(0, 16, middle, 0, unroll=2)
    blocks_on_sublanes(zh_ref, zl_ref, hi_ref, lo_ref, y_ref)

    def sending(s):
        return pltpu.make_async_copy(out_ref.at[:, s], out_hbm.at[:, s], sems.at[s])

    def backward(s, carry):
        at = pl.ds(pl.multiple_of(s * 16, 16), 16)
        for q, (re, im) in enumerate(load(at)):
            out_ref[q, s, 0:16, :] = re
            out_ref[q, s, 16:32, :] = im
        sending(s).start()
        return carry

    lax.fori_loop(0, 16, backward, 0, unroll=2)
    for s in range(16):
        sending(s).wait()


def third_kernel(
    in_hbm, weight_ref, hi_ref, lo_ref, out0, out1, out2, out3,
    x_ref, t_ref, zh_ref, zl_ref, y_ref, i_ref, sems,
):
    m = lax.axis_index("modes")

    def arrival(t):
        return pltpu.make_async_copy(in_hbm.at[pl.ds(t * 8, 8)], x_ref.at[pl.ds(t * 8, 8)], sems.at[t])

    for t in range(16):
        arrival(t).start()

    def unpack(t, carry):
        arrival(t).wait()
        for c in range(2):
            values = [x_ref[t * 8 + s, c * 16 : c * 16 + 16, :] for s in range(8)]
            for k, value in enumerate(swap_groups(values)):
                t_ref[t, c, k] = value
        return carry

    lax.fori_loop(0, 16, unpack, 0, unroll=2)

    def forward(i, carry):
        mode, h = i // 2, i % 2
        xs = [(t_ref[q * 2 + h, 0, mode], t_ref[q * 2 + h, 1, mode]) for q in range(RADIX)]
        for j, pair in enumerate(butterfly(xs)):
            for c in range(2):
                at = pl.ds(pl.multiple_of(c * 128 + mode * 16, 16), 16)
                high, low = split(pair[c])
                zh_ref[j, h, at, :] = high
                zl_ref[j, h, at, :] = low
        return carry

    lax.fori_loop(0, 16, forward, 0, unroll=2)
    blocks_on_lanes(128, zh_ref, zl_ref, hi_ref, lo_ref, y_ref)
    for t in range(16):
        i_ref[t] = jnp.zeros((16, LANES), jnp.float32)

    def backward(i, carry):
        mode, h = i // 2, i % 2
        at = pl.ds(pl.multiple_of(mode * 16, 16), 16)
        weight = weight_ref[jnp.bitwise_xor(m, mode // 2), mode % 2]
        ys = [(y_ref[j, 0, h, at, :], y_ref[j, 1, h, at, :]) for j in range(RADIX)]
        for q, (re, im) in enumerate(unbutterfly(ys)):
            i_ref[q * 2 + h] += weight * (re * re + im * im)
        return carry

    lax.fori_loop(0, 16, backward, 0, unroll=2)
    for k, out_ref in enumerate((out0, out1, out2, out3)):
        owner = jnp.bitwise_xor(m, k)
        for t in range(4):
            out_ref[:, t * LANES : (t + 1) * LANES] = i_ref[owner * 4 + t]


def last_kernel(in0, in1, in2, in3, out_ref):
    m = lax.axis_index("modes")
    for k, in_ref in enumerate((in0, in1, in2, in3)):
        row = pl.multiple_of(jnp.bitwise_xor(m, k) * 16, 16)
        out_ref[pl.ds(row, 16), :] = in_ref[...]


def f32(*shape):
    return jax.ShapeDtypeStruct(shape, jnp.float32)


def exchange(value):
    return lax.all_to_all(value, BOTH, split_axis=0, concat_axis=0, tiled=True)


def partner(value, k):
    return lax.ppermute(value, "modes", [(i, i ^ k) for i in range(4)])


def shards(screens, weights):
    high, low = (jnp.asarray(table) for table in block_tables())
    profiles = jnp.asarray(profile_table())
    vmem = pl.BlockSpec(memory_space=pltpu.VMEM)
    smem = pl.BlockSpec(memory_space=pltpu.SMEM)
    hbm = pl.BlockSpec(memory_space=pltpu.HBM)
    dma = pltpu.SemaphoreType.DMA
    table = pltpu.VMEM((RADIX, 2, 384, LANES), jnp.bfloat16)

    def scratch(*shape, kind=jnp.float32):
        return pltpu.VMEM(shape, kind)

    def halves(rows):
        return [scratch(RADIX, 2, rows, LANES, kind=jnp.bfloat16)] * 2

    mine = weights.reshape(1, 2)
    everyone = jnp.concatenate([mine] + [partner(mine, k) for k in (1, 2, 3)])

    sent = pl.pallas_call(
        first_kernel,
        out_shape=f32(128 * MSG, LANES),
        in_specs=[hbm, vmem, hbm, hbm],
        out_specs=hbm,
        scratch_shapes=[
            scratch(128 * MSG, LANES),
            scratch(2, 16, N),
            scratch(256, LANES),
            table,
            table,
            scratch(2, 16, 16, LANES),
            *halves(128),
            scratch(RADIX, 2, 2, 64, LANES),
            scratch(16, 8, 16, LANES),
            dma((2,)),
            dma((2, RADIX)),
            dma((16,)),
        ],
        name="first",
        compiler_params=params(60),
    )(screens, profiles, high, low)
    got = exchange(sent.reshape(128 * MSG, 1, LANES)).reshape(128 * MSG, LANES)

    sent = pl.pallas_call(
        second_kernel,
        out_shape=f32(RADIX, 16, 32, LANES),
        in_specs=[vmem] * 3,
        out_specs=hbm,
        scratch_shapes=[
            scratch(256, LANES),
            scratch(2, N, LANES),
            *halves(256),
            scratch(RADIX, 2, 256, LANES),
            scratch(RADIX, 16, 32, LANES),
            dma((16,)),
        ],
        name="second",
        compiler_params=params(48),
    )(got, high, low)
    got = exchange(sent.reshape(128, 32, LANES))

    pieces = pl.pallas_call(
        third_kernel,
        out_shape=[f32(16, 512)] * 4,
        in_specs=[hbm, smem, vmem, vmem],
        out_specs=[vmem] * 4,
        scratch_shapes=[
            scratch(128, 32, LANES),
            scratch(16, 2, 8, 16, LANES),
            *halves(256),
            scratch(RADIX, 2, 2, 128, LANES),
            scratch(16, 16, LANES),
            dma((16,)),
        ],
        name="third",
        compiler_params=params(40),
    )(got, everyone, high, low)
    pieces = [pieces[0]] + [partner(pieces[k], k) for k in (1, 2, 3)]

    return pl.pallas_call(
        last_kernel,
        out_shape=f32(64, 512),
        in_specs=[vmem] * 4,
        out_specs=vmem,
        name="last",
        compiler_params=params(24),
    )(*pieces)


def solution(mesh):
    return jax.shard_map(
        shards,
        mesh=mesh,
        in_specs=(P(None, "rows", None), P("modes")),
        out_specs=P("rows", "modes"),
        check_vma=False,
    )
```

```python
import math

import jax
import jax.numpy as jnp
import numpy as np
from jax import lax
from jax.experimental import pallas as pl
from jax.experimental.pallas import tpu as pltpu
from jax.sharding import PartitionSpec as P

N = 2048
RADIX = 8
BLOCK = N // RADIX
LANES = 128
GROUP = 16
MSG = 18
BOTH = ("rows", "modes")
AMPLITUDE = math.sqrt(8.0 / math.sqrt(math.pi / 2.0))
HALF = math.sqrt(0.5)


def params(mib):
    return pltpu.CompilerParams(vmem_limit_bytes=mib * 2**20)


def block_tables():
    freq = np.arange(N)
    signed = np.where(freq >= N // 2, freq - N, freq)
    transfer = np.exp(-2j * np.pi * ((signed * signed) % (8 * N)) / (8 * N))
    offset = np.arange(384)[:, None] - 128 - np.arange(LANES)[None, :]
    bands = np.zeros((RADIX, 2, 384, LANES), np.float64)
    for j in range(RADIX):
        shifted = np.zeros(N, np.complex128)
        shifted[j::RADIX] = transfer[j::RADIX]
        impulse = np.fft.ifft(shifted)
        band = impulse[offset % N]
        bands[j, 0] = band.real
        bands[j, 1] = band.imag
    high = bands.astype(np.float32).astype(jnp.bfloat16)
    low = (bands - high.astype(np.float64)).astype(np.float32).astype(jnp.bfloat16)
    return high, low


def profile_table():
    coord = (np.arange(N) - (N / 2 - 0.5)) / (N / 8)
    scaled = coord * math.sqrt(2.0)
    polys = [np.ones_like(coord), 2.0 * scaled]
    for level in range(1, 3):
        polys.append(2.0 * scaled * polys[level] - 2.0 * level * polys[level - 1])
    rows = []
    for level in range(4):
        norm = math.sqrt(2.0**level * math.factorial(level))
        rows.append(polys[level] * np.exp(-coord * coord) * AMPLITUDE / norm)
    return np.stack(rows).astype(np.float32).reshape(4, 1, N)


def butterfly(x):
    def add(u, v):
        return (u[0] + v[0], u[1] + v[1])

    def sub(u, v):
        return (u[0] - v[0], u[1] - v[1])

    def down(u):
        return (u[1], -u[0])

    a = [add(x[q], x[q + 4]) for q in range(4)]
    b = [sub(x[q], x[q + 4]) for q in range(4)]
    c0, c1 = add(a[0], a[2]), sub(a[0], a[2])
    d0, d1 = add(a[1], a[3]), down(sub(a[1], a[3]))
    e1 = ((b[1][0] + b[1][1]) * HALF, (b[1][1] - b[1][0]) * HALF)
    e3 = ((b[3][1] - b[3][0]) * HALF, (b[3][0] + b[3][1]) * -HALF)
    e2 = down(b[2])
    f0, f1 = add(b[0], e2), sub(b[0], e2)
    g0, g1 = add(e1, e3), down(sub(e1, e3))
    return [
        add(c0, d0),
        add(f0, g0),
        add(c1, d1),
        add(f1, g1),
        sub(c0, d0),
        sub(f0, g0),
        sub(c1, d1),
        sub(f1, g1),
    ]


def unbutterfly(y):
    return [(z[1], z[0]) for z in butterfly([(v[1], v[0]) for v in y])]


def sincos(x):
    turns = jnp.floor(x * (2.0 / math.pi) + 0.5)
    r = x - turns * 1.5703125
    r = r - turns * 4.837512969970703125e-4
    r = r - turns * 7.54978995489188216e-8
    quadrant = turns.astype(jnp.int32)
    z = r * r
    s = ((-1.9515295891e-4 * z + 8.3321608736e-3) * z - 1.6666654611e-1) * z * r + r
    c = ((2.443315711809948e-5 * z - 1.388731625493765e-3) * z + 4.166664568298827e-2) * z * z
    c = c - 0.5 * z + 1.0
    odd = (quadrant & 1) == 1
    sine = jnp.where(odd, c, s)
    cosine = jnp.where(odd, s, c)
    sine = jnp.where((quadrant & 2) == 2, -sine, sine)
    cosine = jnp.where(((quadrant + 1) & 2) == 2, -cosine, cosine)
    return sine, cosine


def split(value):
    high = value.astype(jnp.bfloat16)
    low = (value - high.astype(jnp.float32)).astype(jnp.bfloat16)
    return high, low


def lane_groups(shape):
    return lax.broadcasted_iota(jnp.int32, shape, 1) // GROUP


def swap_groups(rows, before=True, after=True):
    groups = lane_groups(rows[0].shape)
    rows = list(rows)
    if before:
        rows = [rows[0]] + [pltpu.roll(rows[k], k * GROUP, 1) for k in range(1, 8)]
    for step in (1, 2, 4):
        moves = (groups & step) != 0
        rows = [jnp.where(moves, rows[(k + step) % 8], rows[k]) for k in range(8)]
    rows = [rows[0]] + [rows[8 - k] for k in range(1, 8)]
    if after:
        rows = [rows[0]] + [pltpu.roll(rows[k], LANES - k * GROUP, 1) for k in range(1, 8)]
    return rows


def matrix(table_ref, j, part):
    return jnp.concatenate(
        [table_ref[j, part, 128:384, :], table_ref[j, part, 0:256, :]], axis=1
    )


def dot(left, right):
    return jnp.dot(left, right, preferred_element_type=jnp.float32)


def blocks_on_lanes(half, zh_ref, zl_ref, hi_ref, lo_ref, y_ref, wait=None):
    def body(j, carry):
        t = lax.rem(RADIX - j, RADIX)
        if wait is not None:
            wait(t)
        zh = jnp.concatenate([zh_ref[j, 0], zh_ref[j, 1]], axis=1)
        zl = jnp.concatenate([zl_ref[j, 0], zl_ref[j, 1]], axis=1)
        wrh, wih = matrix(hi_ref, t, 0), matrix(hi_ref, t, 1)
        wrl, wil = matrix(lo_ref, t, 0), matrix(lo_ref, t, 1)
        both = jnp.concatenate([zh, zl], axis=0)
        pr = dot(both, wrh)
        pr = pr[: 2 * half] + pr[2 * half :] + dot(zh, wrl)
        pi = dot(both, wih)
        pi = pi[: 2 * half] + pi[2 * half :] + dot(zh, wil)
        re = pr[:half] - pi[half:]
        im = pi[:half] + pr[half:]
        for h in range(2):
            y_ref[j, 0, h] = re[:, h * LANES : (h + 1) * LANES]
            y_ref[j, 1, h] = im[:, h * LANES : (h + 1) * LANES]
        return carry

    lax.fori_loop(0, RADIX, body, 0)


def blocks_on_sublanes(zh_ref, zl_ref, hi_ref, lo_ref, y_ref):
    def body(j, carry):
        zh = jnp.concatenate([zh_ref[j, 0], zh_ref[j, 1]], axis=1)
        zl = jnp.concatenate([zl_ref[j, 0], zl_ref[j, 1]], axis=1)
        brh, bih = matrix(hi_ref, j, 0), matrix(hi_ref, j, 1)
        brl, bil = matrix(lo_ref, j, 0), matrix(lo_ref, j, 1)
        tr = dot(brh, zh) + dot(brl, zh) + dot(brh, zl)
        ti = dot(bih, zh) + dot(bil, zh) + dot(bih, zl)
        y_ref[j, 0] = tr[:, :LANES] - ti[:, LANES:]
        y_ref[j, 1] = tr[:, LANES:] + ti[:, :LANES]
        return carry

    lax.fori_loop(0, RADIX, body, 0)


def first_kernel(
    screens_ref,
    prof_hbm,
    hi_hbm,
    lo_hbm,
    out_hbm,
    prof_ref,
    out_ref,
    s_ref,
    e_ref,
    hi_ref,
    lo_ref,
    cs_ref,
    zh_ref,
    zl_ref,
    y_ref,
    t_ref,
    screen_sems,
    table_sems,
    out_sems,
):
    m = lax.axis_index("modes")
    r = lax.axis_index("rows")
    rows = pl.ds(pl.multiple_of(m * 16, 16), 16)

    def screen_copy(k):
        return pltpu.make_async_copy(
            screens_ref.at[k, rows, :], s_ref.at[k], screen_sems.at[k]
        )

    def table_copies(t):
        return [
            pltpu.make_async_copy(hi_hbm.at[t], hi_ref.at[t], table_sems.at[0, t]),
            pltpu.make_async_copy(lo_hbm.at[t], lo_ref.at[t], table_sems.at[1, t]),
        ]

    prof_copy = pltpu.make_async_copy(prof_hbm, prof_ref, screen_sems.at[2])
    screen_copy(0).start()
    prof_copy.start()
    screen_copy(1).start()
    for j in range(RADIX):
        for copy in table_copies((RADIX - j) % RADIX):
            copy.start()

    cell = lax.broadcasted_iota(jnp.int32, (16, LANES), 0) + (r * 64 + m * 16)
    coord = (cell.astype(jnp.float32) - (N / 2 - 0.5)) / (N / 8)
    envelope = jnp.exp(-coord * coord) * AMPLITUDE
    screen_copy(0).wait()

    def screens(t, carry):
        lanes = pl.ds(pl.multiple_of(t * LANES, LANES), LANES)
        sine, cosine = sincos(s_ref[0, :, lanes])
        cs_ref[0, t] = cosine * envelope
        cs_ref[1, t] = sine * envelope
        return carry

    lax.fori_loop(0, 16, screens, 0, unroll=4)
    prof_copy.wait()

    def forward(i, carry):
        b, h = i // 2, i % 2
        xs = []
        for q in range(RADIX):
            at = pl.ds(pl.multiple_of(q * BLOCK + h * LANES, LANES), LANES)
            weight = prof_ref[b, :, at]
            xs.append((cs_ref[0, q * 2 + h] * weight, cs_ref[1, q * 2 + h] * weight))
        for j, pair in enumerate(butterfly(xs)):
            for c in range(2):
                at = pl.ds(pl.multiple_of(c * 64 + b * 16, 16), 16)
                high, low = split(pair[c])
                zh_ref[j, h, at, :] = high
                zl_ref[j, h, at, :] = low
        return carry

    lax.fori_loop(0, 8, forward, 0, unroll=2)

    def wait(t):
        for copy in table_copies(t):
            copy.wait()

    blocks_on_lanes(64, zh_ref, zl_ref, hi_ref, lo_ref, y_ref, wait)

    def backward(i, carry):
        b, h = i // 2, i % 2
        at = pl.ds(pl.multiple_of(b * 16, 16), 16)
        ys = [(y_ref[j, 0, h, at, :], y_ref[j, 1, h, at, :]) for j in range(RADIX)]
        for q, pair in enumerate(unbutterfly(ys)):
            t_ref[q * 2 + h, b] = pair[0]
            t_ref[q * 2 + h, 4 + b] = pair[1]
        return carry

    lax.fori_loop(0, 8, backward, 0, unroll=2)
    screen_copy(1).wait()

    def lines(t, carry):
        lanes = pl.ds(pl.multiple_of(t * LANES, LANES), LANES)
        e_ref[pl.ds(pl.multiple_of(t * 16, 16), 16), :] = s_ref[1, :, lanes]
        return carry

    lax.fori_loop(0, 16, lines, 0, unroll=4)
    for t in range(0, 16, 4):
        values = [e_ref[pl.ds(t * 16 + g, 8, stride=8), :] for g in range(8)]
        for k, value in enumerate(swap_groups(values)):
            for u in range(4):
                at = ((t + u) * 8 + k) * MSG + 16
                out_ref[at : at + 2, :] = value[2 * u : 2 * u + 2, :]

    def sending(t):
        at = pl.ds(pl.multiple_of(t * (8 * MSG), 8), 8 * MSG)
        return pltpu.make_async_copy(out_ref.at[at, :], out_hbm.at[at, :], out_sems.at[t])

    def pack(t, carry):
        for k, value in enumerate(swap_groups([t_ref[t, k] for k in range(8)], after=False)):
            out_ref[pl.ds((t * 8 + k) * MSG, 16), :] = value
        sending(t).start()
        return carry

    lax.fori_loop(0, 16, pack, 0, unroll=4)
    for t in range(16):
        sending(t).wait()


def second_kernel(
    in_ref, hi_ref, lo_ref, out_hbm, p_ref, e_ref, zh_ref, zl_ref, y_ref, out_ref, sems
):
    groups = lane_groups((8, LANES))

    def gather(p, carry):
        for u in range(8):
            p_ref[pl.ds(p * 16 + u * 2, 2), :] = in_ref[pl.ds(p * (8 * MSG) + u * MSG + 16, 2), :]
        return carry

    lax.fori_loop(0, 16, gather, 0, unroll=4)

    def phases(p, carry):
        packed = p_ref[pl.ds(pl.multiple_of(p * 8, 8), 8), :]
        sine, cosine = sincos(packed)
        for c, value in enumerate((cosine, sine)):
            level = [value]
            for step in (4, 2, 1):
                keep = (groups & step) == 0
                following = []
                for value in level:
                    moved = pltpu.roll(value, step * GROUP, 1)
                    following.append(jnp.where(keep, value, moved))
                    following.append(jnp.where(keep, moved, value))
                level = following
            for k in range(8):
                e_ref[c, pl.ds(p * 64 + k, 8, stride=8), :] = level[k]
        return carry

    lax.fori_loop(0, 32, phases, 0, unroll=4)
    turn = (lax.axis_index("rows") * 4 + lax.axis_index("modes")) % 8
    left = ((lane_groups((16, LANES)) - turn + 8) & 7) < 4
    line = lax.broadcasted_iota(jnp.int32, (16, LANES), 0).astype(jnp.float32)
    line = (line - (N / 2 - 0.5)) * (2.0 / (N / 8))

    def store(at, pairs):
        for j, pair in enumerate(pairs):
            for c in range(2):
                high, low = split(pair[c])
                zh_ref[j, c, at, :] = high
                zl_ref[j, c, at, :] = low

    def load(at):
        return unbutterfly([(y_ref[j, 0, at, :], y_ref[j, 1, at, :]) for j in range(RADIX)])

    def forward(s, carry):
        start = (s * 16).astype(jnp.float32) * (2.0 / (N / 8))
        xs = []
        for q in range(RADIX):
            value = in_ref[pl.ds((s + q * 16) * MSG, 16), :]
            moved = pltpu.roll(value, 64, 1)
            factor = jnp.where(left, 1.0, line + (start + q * BLOCK * (2.0 / (N / 8))))
            xs.append((jnp.where(left, value, moved) * factor, jnp.where(left, moved, value) * factor))
        store(pl.ds(pl.multiple_of(s * 16, 16), 16), butterfly(xs))
        return carry

    lax.fori_loop(0, 16, forward, 0, unroll=2)
    blocks_on_sublanes(zh_ref, zl_ref, hi_ref, lo_ref, y_ref)

    def middle(s, carry):
        at = pl.ds(pl.multiple_of(s * 16, 16), 16)
        xs = []
        for q, (re, im) in enumerate(load(at)):
            here = pl.ds(pl.multiple_of(s * 16 + q * BLOCK, 16), 16)
            cosine, sine = e_ref[0, here, :], e_ref[1, here, :]
            xs.append((re * cosine - im * sine, re * sine + im * cosine))
        store(at, butterfly(xs))
        return carry

    lax.fori_loop(0, 16, middle, 0, unroll=2)
    blocks_on_sublanes(zh_ref, zl_ref, hi_ref, lo_ref, y_ref)

    def sending(s):
        return pltpu.make_async_copy(out_ref.at[:, s], out_hbm.at[:, s], sems.at[s])

    def backward(s, carry):
        at = pl.ds(pl.multiple_of(s * 16, 16), 16)
        for q, (re, im) in enumerate(load(at)):
            out_ref[q, s, 0:16, :] = re
            out_ref[q, s, 16:32, :] = im
        sending(s).start()
        return carry

    lax.fori_loop(0, 16, backward, 0, unroll=2)
    for s in range(16):
        sending(s).wait()


def third_kernel(
    in_hbm, weight_ref, hi_ref, lo_ref, out0, out1, out2, out3,
    x_ref, t_ref, zh_ref, zl_ref, y_ref, i_ref, sems,
):
    m = lax.axis_index("modes")

    def arrival(t):
        return pltpu.make_async_copy(in_hbm.at[pl.ds(t * 8, 8)], x_ref.at[pl.ds(t * 8, 8)], sems.at[t])

    for t in range(16):
        arrival(t).start()

    def unpack(t, carry):
        arrival(t).wait()
        for c in range(2):
            values = [x_ref[t * 8 + s, c * 16 : c * 16 + 16, :] for s in range(8)]
            for k, value in enumerate(swap_groups(values, before=False)):
                t_ref[t, c, k] = value
        return carry

    lax.fori_loop(0, 16, unpack, 0, unroll=2)

    def forward(i, carry):
        mode, h = i // 2, i % 2
        xs = [(t_ref[q * 2 + h, 0, mode], t_ref[q * 2 + h, 1, mode]) for q in range(RADIX)]
        for j, pair in enumerate(butterfly(xs)):
            for c in range(2):
                at = pl.ds(pl.multiple_of(c * 128 + mode * 16, 16), 16)
                high, low = split(pair[c])
                zh_ref[j, h, at, :] = high
                zl_ref[j, h, at, :] = low
        return carry

    lax.fori_loop(0, 16, forward, 0, unroll=2)
    blocks_on_lanes(128, zh_ref, zl_ref, hi_ref, lo_ref, y_ref)
    for t in range(16):
        i_ref[t] = jnp.zeros((16, LANES), jnp.float32)

    def backward(i, carry):
        mode, h = i // 2, i % 2
        at = pl.ds(pl.multiple_of(mode * 16, 16), 16)
        weight = weight_ref[jnp.bitwise_xor(m, mode // 2) * 2 + mode % 2]
        ys = [(y_ref[j, 0, h, at, :], y_ref[j, 1, h, at, :]) for j in range(RADIX)]
        for q, (re, im) in enumerate(unbutterfly(ys)):
            i_ref[q * 2 + h] += weight * (re * re + im * im)
        return carry

    lax.fori_loop(0, 16, backward, 0, unroll=2)
    for k, out_ref in enumerate((out0, out1, out2, out3)):
        owner = jnp.bitwise_xor(m, k)
        for t in range(4):
            out_ref[:, t * LANES : (t + 1) * LANES] = i_ref[owner * 4 + t]


def last_kernel(in0, in1, in2, in3, out_ref):
    m = lax.axis_index("modes")
    for k, in_ref in enumerate((in0, in1, in2, in3)):
        row = pl.multiple_of(jnp.bitwise_xor(m, k) * 16, 16)
        out_ref[pl.ds(row, 16), :] = in_ref[...]


def f32(*shape):
    return jax.ShapeDtypeStruct(shape, jnp.float32)


def exchange(value):
    return lax.all_to_all(value, BOTH, split_axis=0, concat_axis=0, tiled=True)


def partner(value, k):
    return lax.ppermute(value, "modes", [(i, i ^ k) for i in range(4)])


def shards(screens, weights):
    high, low = (jnp.asarray(table) for table in block_tables())
    profiles = jnp.asarray(profile_table())
    vmem = pl.BlockSpec(memory_space=pltpu.VMEM)
    hbm = pl.BlockSpec(memory_space=pltpu.HBM)
    dma = pltpu.SemaphoreType.DMA
    table = pltpu.VMEM((RADIX, 2, 384, LANES), jnp.bfloat16)

    def scratch(*shape, kind=jnp.float32):
        return pltpu.VMEM(shape, kind)

    def halves(rows):
        return [scratch(RADIX, 2, rows, LANES, kind=jnp.bfloat16)] * 2

    mine = weights.reshape(1, 2)
    everyone = jnp.concatenate([mine] + [partner(mine, k) for k in (1, 2, 3)])
    everyone = jnp.broadcast_to(everyone.reshape(8, 1, 1), (8, 1, LANES))

    sent = pl.pallas_call(
        first_kernel,
        out_shape=f32(128 * MSG, LANES),
        in_specs=[hbm] * 4,
        out_specs=hbm,
        scratch_shapes=[
            scratch(4, 1, N),
            scratch(128 * MSG, LANES),
            scratch(2, 16, N),
            scratch(256, LANES),
            table,
            table,
            scratch(2, 16, 16, LANES),
            *halves(128),
            scratch(RADIX, 2, 2, 64, LANES),
            scratch(16, 8, 16, LANES),
            dma((3,)),
            dma((2, RADIX)),
            dma((16,)),
        ],
        name="first",
        compiler_params=params(60),
    )(screens, profiles, high, low)
    got = exchange(sent.reshape(128 * MSG, 1, LANES)).reshape(128 * MSG, LANES)

    sent = pl.pallas_call(
        second_kernel,
        out_shape=f32(RADIX, 16, 32, LANES),
        in_specs=[vmem] * 3,
        out_specs=hbm,
        scratch_shapes=[
            scratch(256, LANES),
            scratch(2, N, LANES),
            *halves(256),
            scratch(RADIX, 2, 256, LANES),
            scratch(RADIX, 16, 32, LANES),
            dma((16,)),
        ],
        name="second",
        compiler_params=params(48),
    )(got, high, low)
    got = exchange(sent.reshape(128, 32, LANES))

    pieces = pl.pallas_call(
        third_kernel,
        out_shape=[f32(16, 512)] * 4,
        in_specs=[hbm, vmem, vmem, vmem],
        out_specs=[vmem] * 4,
        scratch_shapes=[
            scratch(128, 32, LANES),
            scratch(16, 2, 8, 16, LANES),
            *halves(256),
            scratch(RADIX, 2, 2, 128, LANES),
            scratch(16, 16, LANES),
            dma((16,)),
        ],
        name="third",
        compiler_params=params(40),
    )(got, everyone, high, low)
    pieces = [pieces[0]] + [partner(pieces[k], k) for k in (1, 2, 3)]

    return pl.pallas_call(
        last_kernel,
        out_shape=f32(64, 512),
        in_specs=[vmem] * 4,
        out_specs=vmem,
        name="last",
        compiler_params=params(24),
    )(*pieces)


def solution(mesh):
    return jax.shard_map(
        shards,
        mesh=mesh,
        in_specs=(P(None, "rows", None), P("modes")),
        out_specs=P("rows", "modes"),
        check_vma=False,
    )
```

```python
import math

import jax
import jax.numpy as jnp
import numpy as np
from jax import lax
from jax.experimental import pallas as pl
from jax.experimental.pallas import tpu as pltpu
from jax.sharding import PartitionSpec as P

N = 2048
RADIX = 8
BLOCK = N // RADIX
LANES = 128
GROUP = 16
MSG = 18
BOTH = ("rows", "modes")
AMPLITUDE = math.sqrt(8.0 / math.sqrt(math.pi / 2.0))
HALF = math.sqrt(0.5)


def params(mib):
    return pltpu.CompilerParams(vmem_limit_bytes=mib * 2**20)


def block_tables():
    freq = np.arange(N)
    signed = np.where(freq >= N // 2, freq - N, freq)
    transfer = np.exp(-2j * np.pi * ((signed * signed) % (8 * N)) / (8 * N))
    offset = np.arange(384)[:, None] - 128 - np.arange(LANES)[None, :]
    bands = np.zeros((RADIX, 2, 384, LANES), np.float64)
    for j in range(RADIX):
        shifted = np.zeros(N, np.complex128)
        shifted[j::RADIX] = transfer[j::RADIX]
        impulse = np.fft.ifft(shifted)
        band = impulse[offset % N]
        bands[j, 0] = band.real
        bands[j, 1] = band.imag
    high = bands.astype(np.float32).astype(jnp.bfloat16)
    low = (bands - high.astype(np.float64)).astype(np.float32).astype(jnp.bfloat16)
    return high, low


def profile_table():
    coord = (np.arange(N) - (N / 2 - 0.5)) / (N / 8)
    scaled = coord * math.sqrt(2.0)
    polys = [np.ones_like(coord), 2.0 * scaled]
    for level in range(1, 3):
        polys.append(2.0 * scaled * polys[level] - 2.0 * level * polys[level - 1])
    rows = []
    for level in range(4):
        norm = math.sqrt(2.0**level * math.factorial(level))
        rows.append(polys[level] * np.exp(-coord * coord) * AMPLITUDE / norm)
    return np.stack(rows).astype(np.float32).reshape(4, 1, N)


def butterfly(x):
    def add(u, v):
        return (u[0] + v[0], u[1] + v[1])

    def sub(u, v):
        return (u[0] - v[0], u[1] - v[1])

    def down(u):
        return (u[1], -u[0])

    a = [add(x[q], x[q + 4]) for q in range(4)]
    b = [sub(x[q], x[q + 4]) for q in range(4)]
    c0, c1 = add(a[0], a[2]), sub(a[0], a[2])
    d0, d1 = add(a[1], a[3]), down(sub(a[1], a[3]))
    e1 = ((b[1][0] + b[1][1]) * HALF, (b[1][1] - b[1][0]) * HALF)
    e3 = ((b[3][1] - b[3][0]) * HALF, (b[3][0] + b[3][1]) * -HALF)
    e2 = down(b[2])
    f0, f1 = add(b[0], e2), sub(b[0], e2)
    g0, g1 = add(e1, e3), down(sub(e1, e3))
    return [
        add(c0, d0),
        add(f0, g0),
        add(c1, d1),
        add(f1, g1),
        sub(c0, d0),
        sub(f0, g0),
        sub(c1, d1),
        sub(f1, g1),
    ]


def unbutterfly(y):
    return [(z[1], z[0]) for z in butterfly([(v[1], v[0]) for v in y])]


def sincos(x):
    turns = jnp.floor(x * (2.0 / math.pi) + 0.5)
    r = x - turns * 1.5703125
    r = r - turns * 4.837512969970703125e-4
    r = r - turns * 7.54978995489188216e-8
    quadrant = turns.astype(jnp.int32)
    z = r * r
    s = ((-1.9515295891e-4 * z + 8.3321608736e-3) * z - 1.6666654611e-1) * z * r + r
    c = ((2.443315711809948e-5 * z - 1.388731625493765e-3) * z + 4.166664568298827e-2) * z * z
    c = c - 0.5 * z + 1.0
    odd = (quadrant & 1) == 1
    sine = jnp.where(odd, c, s)
    cosine = jnp.where(odd, s, c)
    sine = jnp.where((quadrant & 2) == 2, -sine, sine)
    cosine = jnp.where(((quadrant + 1) & 2) == 2, -cosine, cosine)
    return sine, cosine


def split(value):
    high = value.astype(jnp.bfloat16)
    low = (value - high.astype(jnp.float32)).astype(jnp.bfloat16)
    return high, low


def lane_groups(shape):
    return lax.broadcasted_iota(jnp.int32, shape, 1) // GROUP


def swap_groups(rows, before=True, after=True):
    groups = lane_groups(rows[0].shape)
    rows = list(rows)
    if before:
        rows = [rows[0]] + [pltpu.roll(rows[k], k * GROUP, 1) for k in range(1, 8)]
    for step in (1, 2, 4):
        moves = (groups & step) != 0
        rows = [jnp.where(moves, rows[(k + step) % 8], rows[k]) for k in range(8)]
    rows = [rows[0]] + [rows[8 - k] for k in range(1, 8)]
    if after:
        rows = [rows[0]] + [pltpu.roll(rows[k], LANES - k * GROUP, 1) for k in range(1, 8)]
    return rows


def matrix(table_ref, j, part):
    return jnp.concatenate(
        [table_ref[j, part, 128:384, :], table_ref[j, part, 0:256, :]], axis=1
    )


def dot(left, right):
    return jnp.dot(left, right, preferred_element_type=jnp.float32)


def block_on_lanes(j, half, zh_ref, zl_ref, hi_ref, lo_ref, y_ref):
    t = lax.rem(RADIX - j, RADIX)
    zh = jnp.concatenate([zh_ref[j, 0], zh_ref[j, 1]], axis=1)
    zl = jnp.concatenate([zl_ref[j, 0], zl_ref[j, 1]], axis=1)
    wrh, wih = matrix(hi_ref, t, 0), matrix(hi_ref, t, 1)
    wrl, wil = matrix(lo_ref, t, 0), matrix(lo_ref, t, 1)
    both = jnp.concatenate([zh, zl], axis=0)
    pr = dot(both, wrh)
    pr = pr[: 2 * half] + pr[2 * half :] + dot(zh, wrl)
    pi = dot(both, wih)
    pi = pi[: 2 * half] + pi[2 * half :] + dot(zh, wil)
    re = pr[:half] - pi[half:]
    im = pi[:half] + pr[half:]
    for h in range(2):
        y_ref[j, 0, h] = re[:, h * LANES : (h + 1) * LANES]
        y_ref[j, 1, h] = im[:, h * LANES : (h + 1) * LANES]


def block_on_sublanes(j, zh_ref, zl_ref, hi_ref, lo_ref, y_ref):
    zh = jnp.concatenate([zh_ref[j, 0], zh_ref[j, 1]], axis=1)
    zl = jnp.concatenate([zl_ref[j, 0], zl_ref[j, 1]], axis=1)
    brh, bih = matrix(hi_ref, j, 0), matrix(hi_ref, j, 1)
    brl, bil = matrix(lo_ref, j, 0), matrix(lo_ref, j, 1)
    tr = dot(brh, zh) + dot(brl, zh) + dot(brh, zl)
    ti = dot(bih, zh) + dot(bil, zh) + dot(bih, zl)
    y_ref[j, 0] = tr[:, :LANES] - ti[:, LANES:]
    y_ref[j, 1] = tr[:, LANES:] + ti[:, :LANES]


def loop(count, body, unroll=1):
    def step(i, carry):
        body(i)
        return carry

    lax.fori_loop(0, count, step, 0, unroll=unroll)


def first_kernel(
    screens_ref,
    prof_hbm,
    hi_hbm,
    lo_hbm,
    out_hbm,
    prof_ref,
    out_ref,
    s_ref,
    e_ref,
    hi_ref,
    lo_ref,
    cs_ref,
    zh_ref,
    zl_ref,
    y_ref,
    t_ref,
    screen_sems,
    table_sems,
    out_sems,
):
    m = lax.axis_index("modes")
    r = lax.axis_index("rows")
    rows = pl.ds(pl.multiple_of(m * 16, 16), 16)

    def screen_copy(k):
        return pltpu.make_async_copy(
            screens_ref.at[k, rows, :], s_ref.at[k], screen_sems.at[k]
        )

    def table_copies(t):
        return [
            pltpu.make_async_copy(hi_hbm.at[t], hi_ref.at[t], table_sems.at[0, t]),
            pltpu.make_async_copy(lo_hbm.at[t], lo_ref.at[t], table_sems.at[1, t]),
        ]

    prof_copy = pltpu.make_async_copy(prof_hbm, prof_ref, screen_sems.at[2])
    screen_copy(0).start()
    prof_copy.start()
    screen_copy(1).start()
    for j in range(RADIX):
        for copy in table_copies((RADIX - j) % RADIX):
            copy.start()

    cell = lax.broadcasted_iota(jnp.int32, (16, LANES), 0) + (r * 64 + m * 16)
    coord = (cell.astype(jnp.float32) - (N / 2 - 0.5)) / (N / 8)
    envelope = jnp.exp(-coord * coord) * AMPLITUDE
    screen_copy(0).wait()

    def screens(t, carry):
        lanes = pl.ds(pl.multiple_of(t * LANES, LANES), LANES)
        sine, cosine = sincos(s_ref[0, :, lanes])
        cs_ref[0, t] = cosine * envelope
        cs_ref[1, t] = sine * envelope
        return carry

    lax.fori_loop(0, 16, screens, 0, unroll=4)
    prof_copy.wait()

    def forward(i, carry):
        b, h = i // 2, i % 2
        xs = []
        for q in range(RADIX):
            at = pl.ds(pl.multiple_of(q * BLOCK + h * LANES, LANES), LANES)
            weight = prof_ref[b, :, at]
            xs.append((cs_ref[0, q * 2 + h] * weight, cs_ref[1, q * 2 + h] * weight))
        for j, pair in enumerate(butterfly(xs)):
            for c in range(2):
                at = pl.ds(pl.multiple_of(c * 64 + b * 16, 16), 16)
                high, low = split(pair[c])
                zh_ref[j, h, at, :] = high
                zl_ref[j, h, at, :] = low
        return carry

    lax.fori_loop(0, 8, forward, 0, unroll=2)

    screen_copy(1).wait()

    def lines(t, carry):
        lanes = pl.ds(pl.multiple_of(t * LANES, LANES), LANES)
        e_ref[pl.ds(pl.multiple_of(t * 16, 16), 16), :] = s_ref[1, :, lanes]
        return carry

    lax.fori_loop(0, 16, lines, 0, unroll=4)

    def products(p):
        for j in (2 * p, 2 * p + 1):
            for copy in table_copies(lax.rem(RADIX - j, RADIX)):
                copy.wait()
        for j in (2 * p, 2 * p + 1):
            block_on_lanes(j, 64, zh_ref, zl_ref, hi_ref, lo_ref, y_ref)
        values = [e_ref[pl.ds(p * 64 + g, 8, stride=8), :] for g in range(8)]
        for k, value in enumerate(swap_groups(values)):
            for u in range(4):
                at = pl.ds(p * (32 * MSG) + ((u * 8 + k) * MSG + 16), 2)
                out_ref[at, :] = value[2 * u : 2 * u + 2, :]

    loop(4, products)

    def backward(i, carry):
        b, h = i // 2, i % 2
        at = pl.ds(pl.multiple_of(b * 16, 16), 16)
        ys = [(y_ref[j, 0, h, at, :], y_ref[j, 1, h, at, :]) for j in range(RADIX)]
        for q, pair in enumerate(unbutterfly(ys)):
            t_ref[q * 2 + h, b] = pair[0]
            t_ref[q * 2 + h, 4 + b] = pair[1]
        return carry

    lax.fori_loop(0, 8, backward, 0, unroll=2)
    def sending(t):
        at = pl.ds(pl.multiple_of(t * (8 * MSG), 8), 8 * MSG)
        return pltpu.make_async_copy(out_ref.at[at, :], out_hbm.at[at, :], out_sems.at[t])

    def pack(t, carry):
        for k, value in enumerate(swap_groups([t_ref[t, k] for k in range(8)], after=False)):
            out_ref[pl.ds((t * 8 + k) * MSG, 16), :] = value
        sending(t).start()
        return carry

    lax.fori_loop(0, 16, pack, 0, unroll=4)
    for t in range(16):
        sending(t).wait()


def second_kernel(
    in_ref, hi_ref, lo_ref, out_hbm, p_ref, e_ref, zh_ref, zl_ref, y_ref, out_ref, sems
):
    groups = lane_groups((8, LANES))

    def gather(p, carry):
        for u in range(8):
            p_ref[pl.ds(p * 16 + u * 2, 2), :] = in_ref[pl.ds(p * (8 * MSG) + u * MSG + 16, 2), :]
        return carry

    lax.fori_loop(0, 16, gather, 0, unroll=4)

    def phases(p):
        packed = p_ref[pl.ds(pl.multiple_of(p * 8, 8), 8), :]
        sine, cosine = sincos(packed)
        for c, value in enumerate((cosine, sine)):
            level = [value]
            for step in (4, 2, 1):
                keep = (groups & step) == 0
                following = []
                for value in level:
                    moved = pltpu.roll(value, step * GROUP, 1)
                    following.append(jnp.where(keep, value, moved))
                    following.append(jnp.where(keep, moved, value))
                level = following
            for k in range(8):
                e_ref[c, pl.ds(p * 64 + k, 8, stride=8), :] = level[k]

    turn = (lax.axis_index("rows") * 4 + lax.axis_index("modes")) % 8
    left = ((lane_groups((16, LANES)) - turn + 8) & 7) < 4
    line = lax.broadcasted_iota(jnp.int32, (16, LANES), 0).astype(jnp.float32)
    line = (line - (N / 2 - 0.5)) * (2.0 / (N / 8))

    def store(at, pairs):
        for j, pair in enumerate(pairs):
            for c in range(2):
                high, low = split(pair[c])
                zh_ref[j, c, at, :] = high
                zl_ref[j, c, at, :] = low

    def load(at):
        return unbutterfly([(y_ref[j, 0, at, :], y_ref[j, 1, at, :]) for j in range(RADIX)])

    def forward(s, carry):
        start = (s * 16).astype(jnp.float32) * (2.0 / (N / 8))
        xs = []
        for q in range(RADIX):
            value = in_ref[pl.ds((s + q * 16) * MSG, 16), :]
            moved = pltpu.roll(value, 64, 1)
            factor = jnp.where(left, 1.0, line + (start + q * BLOCK * (2.0 / (N / 8))))
            xs.append((jnp.where(left, value, moved) * factor, jnp.where(left, moved, value) * factor))
        store(pl.ds(pl.multiple_of(s * 16, 16), 16), butterfly(xs))
        return carry

    lax.fori_loop(0, 16, forward, 0, unroll=2)

    def products(j):
        block_on_sublanes(j, zh_ref, zl_ref, hi_ref, lo_ref, y_ref)
        for u in range(4):
            phases(j * 4 + u)

    loop(RADIX, products)

    def middle(s, carry):
        at = pl.ds(pl.multiple_of(s * 16, 16), 16)
        xs = []
        for q, (re, im) in enumerate(load(at)):
            here = pl.ds(pl.multiple_of(s * 16 + q * BLOCK, 16), 16)
            cosine, sine = e_ref[0, here, :], e_ref[1, here, :]
            xs.append((re * cosine - im * sine, re * sine + im * cosine))
        store(at, butterfly(xs))
        return carry

    lax.fori_loop(0, 16, middle, 0, unroll=2)
    loop(RADIX, lambda j: block_on_sublanes(j, zh_ref, zl_ref, hi_ref, lo_ref, y_ref))

    def sending(s):
        return pltpu.make_async_copy(out_ref.at[:, s], out_hbm.at[:, s], sems.at[s])

    def backward(s, carry):
        at = pl.ds(pl.multiple_of(s * 16, 16), 16)
        for q, (re, im) in enumerate(load(at)):
            out_ref[q, s, 0:16, :] = re
            out_ref[q, s, 16:32, :] = im
        sending(s).start()
        return carry

    lax.fori_loop(0, 16, backward, 0, unroll=2)
    for s in range(16):
        sending(s).wait()


def third_kernel(
    in_hbm, weight_ref, hi_ref, lo_ref, out0, out1, out2, out3,
    x_ref, t_ref, zh_ref, zl_ref, y_ref, i_ref, sems,
):
    m = lax.axis_index("modes")

    def arrival(t):
        return pltpu.make_async_copy(in_hbm.at[pl.ds(t * 8, 8)], x_ref.at[pl.ds(t * 8, 8)], sems.at[t])

    for t in range(16):
        arrival(t).start()

    def unpack(t, carry):
        arrival(t).wait()
        for c in range(2):
            values = [x_ref[t * 8 + s, c * 16 : c * 16 + 16, :] for s in range(8)]
            for k, value in enumerate(swap_groups(values, before=False)):
                t_ref[t, c, k] = value
        return carry

    lax.fori_loop(0, 16, unpack, 0, unroll=2)

    for t in range(16):
        i_ref[t] = jnp.zeros((16, LANES), jnp.float32)

    def forward(i):
        mode, h = i // 2, i % 2
        xs = [(t_ref[q * 2 + h, 0, mode], t_ref[q * 2 + h, 1, mode]) for q in range(RADIX)]
        for j, pair in enumerate(butterfly(xs)):
            for c in range(2):
                at = pl.ds(pl.multiple_of(c * 128 + mode * 16, 16), 16)
                high, low = split(pair[c])
                zh_ref[j, h, at, :] = high
                zl_ref[j, h, at, :] = low

    def backward(i):
        mode, h = i // 2, i % 2
        at = pl.ds(pl.multiple_of(mode * 16, 16), 16)
        weight = weight_ref[jnp.bitwise_xor(m, mode // 2) * 2 + mode % 2]
        ys = [(y_ref[j, 0, h, at, :], y_ref[j, 1, h, at, :]) for j in range(RADIX)]
        for q, (re, im) in enumerate(unbutterfly(ys)):
            i_ref[q * 2 + h] += weight * (re * re + im * im)

    loop(16, forward, unroll=2)
    loop(RADIX, lambda j: block_on_lanes(j, 128, zh_ref, zl_ref, hi_ref, lo_ref, y_ref))
    loop(16, backward, unroll=2)
    for k, out_ref in enumerate((out0, out1, out2, out3)):
        owner = jnp.bitwise_xor(m, k)
        for t in range(4):
            out_ref[:, t * LANES : (t + 1) * LANES] = i_ref[owner * 4 + t]


def last_kernel(in0, in1, in2, in3, out_ref):
    m = lax.axis_index("modes")
    for k, in_ref in enumerate((in0, in1, in2, in3)):
        row = pl.multiple_of(jnp.bitwise_xor(m, k) * 16, 16)
        out_ref[pl.ds(row, 16), :] = in_ref[...]


def f32(*shape):
    return jax.ShapeDtypeStruct(shape, jnp.float32)


def exchange(value):
    return lax.all_to_all(value, BOTH, split_axis=0, concat_axis=0, tiled=True)


def partner(value, k):
    return lax.ppermute(value, "modes", [(i, i ^ k) for i in range(4)])


def shards(screens, weights):
    high, low = (jnp.asarray(table) for table in block_tables())
    profiles = jnp.asarray(profile_table())
    vmem = pl.BlockSpec(memory_space=pltpu.VMEM)
    hbm = pl.BlockSpec(memory_space=pltpu.HBM)
    dma = pltpu.SemaphoreType.DMA
    table = pltpu.VMEM((RADIX, 2, 384, LANES), jnp.bfloat16)

    def scratch(*shape, kind=jnp.float32):
        return pltpu.VMEM(shape, kind)

    def halves(rows):
        return [scratch(RADIX, 2, rows, LANES, kind=jnp.bfloat16)] * 2

    mine = weights.reshape(1, 2)
    everyone = jnp.concatenate([mine] + [partner(mine, k) for k in (1, 2, 3)])
    everyone = jnp.broadcast_to(everyone.reshape(8, 1, 1), (8, 1, LANES))

    sent = pl.pallas_call(
        first_kernel,
        out_shape=f32(128 * MSG, LANES),
        in_specs=[hbm] * 4,
        out_specs=hbm,
        scratch_shapes=[
            scratch(4, 1, N),
            scratch(128 * MSG, LANES),
            scratch(2, 16, N),
            scratch(256, LANES),
            table,
            table,
            scratch(2, 16, 16, LANES),
            *halves(128),
            scratch(RADIX, 2, 2, 64, LANES),
            scratch(16, 8, 16, LANES),
            dma((3,)),
            dma((2, RADIX)),
            dma((16,)),
        ],
        name="first",
        compiler_params=params(60),
    )(screens, profiles, high, low)
    got = exchange(sent.reshape(128 * MSG, 1, LANES)).reshape(128 * MSG, LANES)

    sent = pl.pallas_call(
        second_kernel,
        out_shape=f32(RADIX, 16, 32, LANES),
        in_specs=[vmem] * 3,
        out_specs=hbm,
        scratch_shapes=[
            scratch(256, LANES),
            scratch(2, N, LANES),
            *halves(256),
            scratch(RADIX, 2, 256, LANES),
            scratch(RADIX, 16, 32, LANES),
            dma((16,)),
        ],
        name="second",
        compiler_params=params(48),
    )(got, high, low)
    got = exchange(sent.reshape(128, 32, LANES))

    pieces = pl.pallas_call(
        third_kernel,
        out_shape=[f32(16, 512)] * 4,
        in_specs=[hbm, vmem, vmem, vmem],
        out_specs=[vmem] * 4,
        scratch_shapes=[
            scratch(128, 32, LANES),
            scratch(16, 2, 8, 16, LANES),
            *halves(256),
            scratch(RADIX, 2, 2, 128, LANES),
            scratch(16, 16, LANES),
            dma((16,)),
        ],
        name="third",
        compiler_params=params(40),
    )(got, everyone, high, low)
    pieces = [pieces[0]] + [partner(pieces[k], k) for k in (1, 2, 3)]

    return pl.pallas_call(
        last_kernel,
        out_shape=f32(64, 512),
        in_specs=[vmem] * 4,
        out_specs=vmem,
        name="last",
        compiler_params=params(24),
    )(*pieces)


def solution(mesh):
    return jax.shard_map(
        shards,
        mesh=mesh,
        in_specs=(P(None, "rows", None), P("modes")),
        out_specs=P("rows", "modes"),
        check_vma=False,
    )
```
